32 devices in a mesh: section: 4 (over y, x), ctx: 8 (over z, core).
Axes of the slice: x: 2, y: 2, z: 4, core: 2. Of those that a mesh axis runs over, the one named last changes fastest.
Arguments:
- fwd_in: bfloat16 [4, 1152, 1024], P('section', 'ctx'), may hold values from -6 to 6
- bwd_saved: bfloat16 [4, 1152, 1024], P('section', 'ctx'), may hold values from -6 to 6
- bwd_cot: bfloat16 [4, 1152, 1024], P('section', 'ctx'), may hold values from -6 to 6
- new_tokens: bfloat16 [1024, 1024], P('ctx'), may hold values from -6 to 6
- loss_cot: bfloat16 [1024, 1024], P('ctx'), may hold values from -6 to 6
- gain: bfloat16 [4, 1024], P('section'), may hold values from 0.099609375 to 1.8984375
- w_query: bfloat16 [4, 1024, 1024], P('section'), may hold values from -2 to 2
- w_keyval: bfloat16 [4, 1024, 512], P('section'), may hold values from -2 to 2
- w_out: bfloat16 [4, 1024, 1024], P('section'), may hold values from -0.1875 to 0.1875
Outputs:
- fwd_next: bfloat16 [4, 1152, 1024], P('section', 'ctx')
- cot_next: bfloat16 [4, 1152, 1024], P('section', 'ctx')
The draws below stay inside these ranges and needn't reach their ends.
All inputs are finite; a program needn't handle non-finite values.
Results may differ from the reference program's by a relative error of at most 0.012.
The reference program's roundings to bfloat16 on the way count: a program that leaves them out, or rounds other values in their place, can miss the bound.
Values may be sent and summed in bfloat16 or wider, within the bound.
A program may use at most 64 MiB of HBM per device.

```python
import jax
import jax.numpy as jnp
from jax import lax

D = 1024
HEADS = 16
KV_HEADS = 4
HEAD_DIM = 64
GROUP = 8
MEM_DEV = 16
SEG_DEV = 128
ROWS_DEV = 144
SEG = 1024
LAYERS = 4
SEGMENTS = 1
ROWS = 1152
N_CTX = 8


def weight_base(key, salt, shape):
    values = jax.random.normal(jax.random.fold_in(key, salt), shape, jnp.float32)
    return jnp.clip(values, -6.0, 6.0) * D ** (-0.5)


def draw_w_query(key, part):
    values = weight_base(key, 7201, (LAYERS, D, HEADS * HEAD_DIM))
    return jnp.clip(values, -2.0, 2.0).astype(jnp.bfloat16)


def draw_w_keyval(key, part):
    values = weight_base(key, 7202, (LAYERS, D, 2 * KV_HEADS * HEAD_DIM))
    return jnp.clip(values, -2.0, 2.0).astype(jnp.bfloat16)


def drawn_rows(key, salt):
    noise = jax.random.normal(jax.random.fold_in(key, salt), (LAYERS, ROWS, D), jnp.float32)
    return jnp.clip(noise, -6.0, 6.0)


def draw_fwd_in(key, part):
    return drawn_rows(key, 7301).astype(jnp.bfloat16)


def draw_bwd_saved(key, part):
    return drawn_rows(key, 7302).astype(jnp.bfloat16)


def block_scale(key, extent, pieces, low, high):
    factor_of = 1.0
    for axis_at, shards_of in pieces:
        heights = jax.random.uniform(jax.random.fold_in(jax.random.fold_in(key, 6), axis_at), (shards_of,), jnp.float32, low / len(pieces), high / len(pieces))
        factor_of = factor_of * jnp.repeat(jnp.exp(heights), extent[axis_at] // shards_of).reshape((-1,) + (1,) * (len(extent) - 1 - axis_at))
    return factor_of


def normal_values(rng, dims, deviation, bound, split=(), kind=jnp.bfloat16):
    entries = jax.random.normal(rng, dims, jnp.float32) * deviation
    if len(split) > 0:
        entries = block_scale(rng, dims, split, -0.22, 0.18) * entries
    return jnp.clip(entries, min=-bound, max=bound).astype(kind)


def setup_inputs(seed: int = 0) -> dict:
    key_list = jax.random.split(jax.random.key(seed), 10)
    fwd_in = draw_fwd_in(jax.random.fold_in(key_list[9], 71), 0)
    bwd_saved = draw_bwd_saved(jax.random.fold_in(key_list[9], 71), 0)
    bwd_cot = normal_values(key_list[2], (LAYERS, ROWS, D), 1.0, 6.0, ((0, 4), (1, 8)))
    new_tokens = normal_values(key_list[3], (SEGMENTS * SEG, D), 1.0, 6.0, ((0, 8),))
    loss_cot = normal_values(key_list[4], (SEGMENTS * SEG, D), 1.0, 6.0, ((0, 8),))
    gain = jnp.clip(1.0 + 0.18 * jax.random.normal(key_list[5], (LAYERS, D), jnp.float32), 0.099609375, 1.8984375).astype(jnp.bfloat16)
    w_query = draw_w_query(jax.random.fold_in(key_list[9], 71), 0)
    w_keyval = draw_w_keyval(jax.random.fold_in(key_list[9], 71), 0)
    w_out = normal_values(key_list[8], (LAYERS, HEADS * HEAD_DIM, D), (HEADS * HEAD_DIM) ** -0.5, 0.1875, ((0, 4),))
    return dict(fwd_in=fwd_in, bwd_saved=bwd_saved, bwd_cot=bwd_cot, new_tokens=new_tokens, loss_cot=loss_cot, gain=gain, w_query=w_query, w_keyval=w_keyval, w_out=w_out)


epsilon = 1e-05

def segment_allowed():
    rows = jnp.arange(GROUP * ROWS_DEV, dtype=jnp.int32)
    block = rows // ROWS_DEV
    inner = rows % ROWS_DEV
    is_memory = inner < MEM_DEV
    position = block * SEG_DEV + inner - MEM_DEV
    return is_memory[None, :] | is_memory[:, None] | (position[None, :] <= position[:, None])

def normalize(hidden):
    values = hidden.astype(jnp.float32)
    scale = lax.rsqrt(lax.optimization_barrier(jnp.mean(values * values, axis=-1, keepdims=True)) + epsilon)
    return (values, scale)

def split_heads(query, keyval):
    rows_q = query.shape[0]
    rows_k = keyval.shape[0]
    shared = HEADS // KV_HEADS
    width = KV_HEADS * HEAD_DIM
    grouped = query.reshape(rows_q, KV_HEADS, shared, HEAD_DIM).transpose(1, 2, 0, 3)
    keys = keyval[:, :width].reshape(rows_k, KV_HEADS, HEAD_DIM).transpose(1, 0, 2)
    values = keyval[:, width:].reshape(rows_k, KV_HEADS, HEAD_DIM).transpose(1, 0, 2)
    return (grouped, keys, values)

def head_probs(q_head, k_head, allowed):
    scores = jnp.einsum('grd,kd->grk', q_head.astype(jnp.float32), k_head.astype(jnp.float32), precision=lax.Precision.HIGHEST) * HEAD_DIM ** (-0.5)
    scores = jnp.where(allowed[None], scores, -1e+30)
    top = lax.optimization_barrier(jnp.max(scores, axis=-1, keepdims=True))
    expd = jnp.exp(scores - top)
    return expd / lax.optimization_barrier(jnp.sum(expd, axis=-1, keepdims=True))

def attend_forward(query, keyval, allowed):
    grouped, keys, values = split_heads(query, keyval)

    def one_head(items):
        q_head, k_head, v_head = items
        weights = head_probs(q_head, k_head, allowed).astype(jnp.bfloat16)
        return jnp.einsum('grk,kd->grd', weights.astype(jnp.float32), v_head.astype(jnp.float32), precision=lax.Precision.HIGHEST)
    outs = lax.map(one_head, (grouped, keys, values))
    return outs.transpose(2, 0, 1, 3).reshape(query.shape[0], HEADS * HEAD_DIM).astype(jnp.bfloat16)

def attend_backward(query, keyval, allowed, grad_mixed):
    grouped, keys, values = split_heads(query, keyval)
    shared = HEADS // KV_HEADS
    grads = grad_mixed.reshape(query.shape[0], KV_HEADS, shared, HEAD_DIM).transpose(1, 2, 0, 3)

    def one_head(items):
        q_head, k_head, v_head, g_head = items
        probs = head_probs(q_head, k_head, allowed)
        weights = probs.astype(jnp.bfloat16)
        dprobs = jnp.einsum('grd,kd->grk', g_head.astype(jnp.float32), v_head.astype(jnp.float32), precision=lax.Precision.HIGHEST)
        delta = lax.optimization_barrier(jnp.sum(dprobs * probs, axis=-1, keepdims=True))
        dscores = (probs * (dprobs - delta) * HEAD_DIM ** (-0.5)).astype(jnp.bfloat16)
        grad_q = jnp.einsum('grk,kd->grd', dscores.astype(jnp.float32), k_head.astype(jnp.float32), precision=lax.Precision.HIGHEST)
        grad_k = jnp.einsum('grk,grd->kd', dscores.astype(jnp.float32), q_head.astype(jnp.float32), precision=lax.Precision.HIGHEST)
        grad_v = jnp.einsum('grk,grd->kd', weights.astype(jnp.float32), g_head.astype(jnp.float32), precision=lax.Precision.HIGHEST)
        return (grad_q, grad_k, grad_v)
    grad_q, grad_k, grad_v = lax.map(one_head, (grouped, keys, values, grads))
    rows_k = keyval.shape[0]
    grad_query = grad_q.transpose(2, 0, 1, 3).reshape(query.shape[0], HEADS * HEAD_DIM).astype(jnp.bfloat16)
    grad_keys = grad_k.transpose(1, 0, 2).reshape(rows_k, KV_HEADS * HEAD_DIM)
    grad_values = grad_v.transpose(1, 0, 2).reshape(rows_k, KV_HEADS * HEAD_DIM)
    return (grad_query, jnp.concatenate([grad_keys, grad_values], axis=1))

def project(hidden, gain_row, w_query, w_keyval):
    values, scale = normalize(hidden)
    normed = (values * scale * gain_row.astype(jnp.float32)).astype(jnp.bfloat16)
    query = jnp.dot(normed, w_query, preferred_element_type=jnp.float32).astype(jnp.bfloat16)
    keyval = jnp.dot(normed, w_keyval, preferred_element_type=jnp.float32).astype(jnp.bfloat16)
    return (values, scale, query, keyval)

def layer_forward(hidden, gain_row, w_query, w_keyval, w_out, allowed):
    values, scale, query, keyval = project(hidden, gain_row, w_query, w_keyval)
    mixed = attend_forward(query, keyval, allowed)
    return (values + jnp.dot(mixed, w_out, preferred_element_type=jnp.float32)).astype(jnp.bfloat16)

def layer_backward(hidden, grad_out, gain_row, w_query, w_keyval, w_out, allowed):
    values, scale, query, keyval = project(hidden, gain_row, w_query, w_keyval)
    grad_mixed = jnp.dot(grad_out, w_out.T, preferred_element_type=jnp.float32).astype(jnp.bfloat16)
    grad_query, grad_kv = attend_backward(query, keyval, allowed, grad_mixed)
    grad_keyval = grad_kv.astype(jnp.bfloat16)
    grad_normed = jnp.dot(grad_query, w_query.T, preferred_element_type=jnp.float32)
    grad_normed = grad_normed + jnp.dot(grad_keyval, w_keyval.T, preferred_element_type=jnp.float32)
    plain = values * scale
    pushed = gain_row.astype(jnp.float32) * grad_normed
    grad_in = grad_out.astype(jnp.float32) + scale * (pushed - plain * lax.optimization_barrier(jnp.mean(pushed * plain, axis=-1, keepdims=True)))
    return grad_in.astype(jnp.bfloat16)

def reference(fwd_in, bwd_saved, bwd_cot, new_tokens, loss_cot, gain, w_query, w_keyval, w_out):
    allowed = segment_allowed()
    rows_seg = GROUP * ROWS_DEV

    def forward_layer(items):
        hidden, gain_row, wq_layer, wkv_layer, wo_layer = items
        segs = hidden.reshape(SEGMENTS, rows_seg, D)
        outs = lax.map(lambda seg: layer_forward(seg, gain_row, wq_layer, wkv_layer, wo_layer, allowed), segs)
        return outs.reshape(ROWS, D)

    def backward_layer(items):
        hidden, grad_out, gain_row, wq_layer, wkv_layer, wo_layer = items
        segs = hidden.reshape(SEGMENTS, rows_seg, D)
        grad_segs = grad_out.reshape(SEGMENTS, rows_seg, D)
        outs = lax.map(lambda pair: layer_backward(pair[0], pair[1], gain_row, wq_layer, wkv_layer, wo_layer, allowed), (segs, grad_segs))
        return outs.reshape(ROWS, D)
    outs = lax.map(forward_layer, (fwd_in, gain, w_query, w_keyval, w_out))
    grads = lax.map(backward_layer, (bwd_saved, bwd_cot, gain, w_query, w_keyval, w_out))
    last_blocks = outs[LAYERS - 1].reshape(N_CTX, ROWS_DEV, D)
    first = jnp.concatenate([last_blocks[:, :MEM_DEV], new_tokens.reshape(N_CTX, SEG_DEV, D)], axis=1)
    fwd_next = jnp.concatenate([first.reshape(1, ROWS, D), outs[:-1]], axis=0)
    first_grads = grads[0].reshape(N_CTX, ROWS_DEV, D)
    last = jnp.concatenate([first_grads[:, :MEM_DEV], loss_cot.reshape(N_CTX, SEG_DEV, D)], axis=1)
    cot_next = jnp.concatenate([grads[1:], last.reshape(1, ROWS, D)], axis=0)
    return (fwd_next, cot_next)
```

```python
import functools

import jax
import jax.numpy as jnp
from jax import lax
from jax.experimental import pallas as pl
from jax.experimental.pallas import tpu as pltpu
from jax.sharding import PartitionSpec as P

HEADS = 16
KV_HEADS = 4
HEAD_DIM = 64
GROUP = 8
PAIR = 2
CHIPS = GROUP // PAIR
LOCAL = KV_HEADS // PAIR
SHARED = HEADS // KV_HEADS
LANES = 128
PIECES = 4

epsilon = 1e-05
far = 1 << 30

bf16 = jnp.bfloat16
f32 = jnp.float32
NT = (((1,), (1,)), ((), ()))
NN = (((1,), (0,)), ((), ()))


def mul(a, b, dims=NN):
    return lax.dot_general(a, b, dims, preferred_element_type=f32)


def kernel(
    sections, mem,
    xf_h, xb_h, cot_h, gain_ref, wq_h, wkv_h, wo_h,
    outf_h, outb_h,
    xf, xb, cot, wq, wkv, wo, normed, kvf, kvb, kvt, qf, qb, gb, kpos,
    sd, ex, cat, acc, gsend, grecv, gsum, stacked, halves, gq_send, gq_all, mix_send, mix_all,
    of, ob,
    local_sem, pair_send, pair_recv, kv_send, kv_recv, gr_send, gr_recv, sec_send, sec_recv,
):
    rows = xf_h.shape[0]
    width = xf_h.shape[1]
    both = PAIR * rows
    total = GROUP * rows
    stack = SHARED * both
    half = width // PAIR
    tokens = rows - mem
    kcols = LOCAL * HEAD_DIM

    ctx = lax.axis_index("ctx")
    section = lax.axis_index("section")
    member = lax.rem(ctx, GROUP)
    base = ctx - member
    core = lax.rem(member, PAIR)
    chip = member // PAIR
    other = 1 - core
    partner = base + chip * PAIR + other

    loads = []
    mine = pl.ds(core * rows, rows)
    for at, (src, dst) in enumerate(
        [
            (xb_h, xb.at[mine]), (wkv_h, wkv), (xf_h, xf.at[mine]),
            (wq_h, wq), (cot_h, cot.at[mine]), (wo_h, wo),
        ]
    ):
        copy = pltpu.make_async_copy(src, dst, local_sem.at[at])
        copy.start()
        loads.append(copy)
    load_xb, load_wkv, load_xf, load_wq, load_cot, load_wo = loads

    after = lax.rem(section + 1, sections)
    before = lax.rem(section + sections - 1, sections)
    barrier = pltpu.get_barrier_semaphore()
    for k in range(1, GROUP):
        pl.semaphore_signal(
            barrier, inc=1, device_id={"ctx": base + lax.rem(member + k, GROUP)},
            device_id_type=pl.DeviceIdType.MESH,
        )
    for neighbour in (after, before):
        pl.semaphore_signal(
            barrier, inc=1, device_id={"section": neighbour},
            device_id_type=pl.DeviceIdType.MESH,
        )
    pl.semaphore_wait(barrier, GROUP + 1)

    def remote(src, dst, send, recv, where):
        return pltpu.make_async_remote_copy(
            src_ref=src, dst_ref=dst, send_sem=send, recv_sem=recv,
            device_id=where, device_id_type=pl.DeviceIdType.MESH,
        )

    theirs = pl.ds(other * rows, rows)

    def pair_copy(at, src, dst):
        copy = remote(src, dst, pair_send.at[at], pair_recv.at[at], {"ctx": partner})
        copy.start()
        return copy

    pair_copies = [
        pair_copy(0, xb_h, xb.at[mine]),
        pair_copy(1, xf_h, xf.at[mine]),
        pair_copy(2, cot_h, cot.at[mine]),
    ]

    def pair_arrived(at, dst):
        remote(dst, dst, pair_send.at[at], pair_recv.at[at], {"ctx": partner}).wait_recv()

    for b in range(GROUP):
        inner = lax.broadcasted_iota(jnp.int32, (rows, LANES), 0)
        kpos[b * rows : (b + 1) * rows, :] = jnp.where(
            inner < mem, -1, b * tokens + inner - mem
        )

    gain = gain_ref[...].astype(f32)

    def norm(x):
        values = x.astype(f32)
        scale = lax.rsqrt(jnp.mean(values * values, axis=-1, keepdims=True) + epsilon)
        return values, scale

    def make_normed(x_ref):
        for b in range(PAIR):
            values, scale = norm(x_ref[b * rows : (b + 1) * rows, :])
            normed[b * rows : (b + 1) * rows, :] = (values * scale * gain).astype(bf16)

    chip_rows = pl.ds(chip * both, both)

    def project_kv(kv_ref, kind):
        keys = mul(normed[...], wkv[:, pl.ds(pl.multiple_of(core * kcols, kcols), kcols)])
        vals = mul(
            normed[...],
            wkv[:, pl.ds(pl.multiple_of(KV_HEADS * HEAD_DIM + core * kcols, kcols), kcols)],
        )
        for g in range(LOCAL):
            lanes = slice(g * HEAD_DIM, (g + 1) * HEAD_DIM)
            kv_ref[g, chip_rows, :] = jnp.concatenate(
                [keys[:, lanes], vals[:, lanes]], axis=1
            ).astype(bf16)
        copies = []
        for g in range(LOCAL):
            for k in range(1, CHIPS):
                to = base + lax.rem(chip + k, CHIPS) * PAIR + core
                copy = remote(
                    kv_ref.at[g, chip_rows], kv_ref.at[g, chip_rows],
                    kv_send.at[kind, g, k], kv_recv.at[kind, g, k], {"ctx": to},
                )
                copy.start()
                copies.append(copy)
        return copies

    def kv_arrived(kv_ref, kind, g):
        for k in range(1, CHIPS):
            source = lax.rem(chip + CHIPS - k, CHIPS)
            place = kv_ref.at[g, pl.ds(source * both, both)]
            remote(
                place, place, kv_send.at[kind, g, k], kv_recv.at[kind, g, k],
                {"ctx": base + source * PAIR + core},
            ).wait_recv()

    def spread(matrix, dst, upper, factor):
        rounded = matrix.astype(bf16).astype(f32) * factor
        zero = jnp.zeros((both, HEAD_DIM), f32)
        for g in range(LOCAL):
            for h in range(SHARED):
                at = (g * SHARED + h) * HEAD_DIM
                piece = rounded[:, at : at + HEAD_DIM]
                parts = [zero, piece] if upper else [piece, zero]
                dst[g, h * both : (h + 1) * both, :] = jnp.concatenate(parts, axis=1).astype(bf16)

    scale_by = HEAD_DIM ** (-0.5)
    my_cols = pl.ds(pl.multiple_of(core * half, half), half)

    load_xb.wait()
    pair_arrived(0, xb.at[theirs])
    make_normed(xb)
    load_wkv.wait()
    kv_copies = project_kv(kvb, 0)
    load_wq.wait()
    spread(mul(normed[...], wq[:, my_cols]), qb, False, scale_by)
    load_xf.wait()
    pair_arrived(1, xf.at[theirs])
    make_normed(xf)
    kv_copies += project_kv(kvf, 1)
    load_cot.wait()
    pair_arrived(2, cot.at[theirs])
    load_wo.wait()
    spread(mul(cot[...], wo[my_cols, :], NT), gb, True, 1.0)
    spread(mul(normed[...], wq[:, my_cols]), qf, False, scale_by)

    step = total // PIECES

    def query_positions(start):
        row = start + lax.broadcasted_iota(jnp.int32, (1, LANES), 1)
        for h in range(1, SHARED):
            row = jnp.where(row >= both, row - both, row)
        block = jnp.where(row >= rows, 1, 0)
        inner = row - block * rows
        return jnp.where(inner < mem, far, (chip * PAIR + block) * tokens + inner - mem)

    def backward_chunk(g, i, carry):
        start = pl.multiple_of(i * LANES, LANES)
        pair = jnp.concatenate([qb[g, pl.ds(start, LANES), :], gb[g, pl.ds(start, LANES), :]], axis=0)
        position = query_positions(start)
        top = None
        for p in range(PIECES):
            part = slice(p * step, (p + 1) * step)
            product = mul(kvb[g, part, :], pair, NT)
            scores = jnp.where(kpos[part, :] <= position, product[:, :LANES], -1e30)
            sd[part, :LANES] = scores
            sd[part, LANES:] = product[:, LANES:]
            peak = jnp.max(scores, axis=0, keepdims=True)
            top = peak if top is None else jnp.maximum(top, peak)
        norm_sum = jnp.zeros((1, LANES), f32)
        delta = jnp.zeros((1, LANES), f32)
        for p in range(PIECES):
            part = slice(p * step, (p + 1) * step)
            expd = jnp.exp(sd[part, :LANES] - top)
            ex[part, :] = expd
            norm_sum += jnp.sum(expd, axis=0, keepdims=True)
            delta += jnp.sum(expd * sd[part, LANES:], axis=0, keepdims=True)
        inverse = 1.0 / norm_sum
        delta = delta * inverse
        for p in range(PIECES):
            part = slice(p * step, (p + 1) * step)
            probs = ex[part, :] * inverse
            cat[part, LANES:] = probs.astype(bf16)
            cat[part, :LANES] = (probs * (sd[part, LANES:] - delta)).astype(bf16)
            acc[g, part, :] += mul(cat[part, :], pair)
        turned = mul(kvt[...], cat[:, :LANES])
        stacked[g, pl.ds(start, LANES), :] = turned.T * scale_by
        return carry

    def forward_chunk(g, i, carry):
        start = pl.multiple_of(i * LANES, LANES)
        queries = qf[g, pl.ds(start, LANES), :]
        position = query_positions(start)
        top = None
        for p in range(PIECES):
            part = slice(p * step, (p + 1) * step)
            product = mul(kvf[g, part, :], queries, NT)
            scores = jnp.where(kpos[part, :] <= position, product, -1e30)
            sd[part, :LANES] = scores
            peak = jnp.max(scores, axis=0, keepdims=True)
            top = peak if top is None else jnp.maximum(top, peak)
        norm_sum = jnp.zeros((1, LANES), f32)
        for p in range(PIECES):
            part = slice(p * step, (p + 1) * step)
            expd = jnp.exp(sd[part, :LANES] - top)
            ex[part, :] = expd
            norm_sum += jnp.sum(expd, axis=0, keepdims=True)
        inverse = 1.0 / norm_sum
        for p in range(PIECES):
            part = slice(p * step, (p + 1) * step)
            cat[part, :LANES] = (ex[part, :] * inverse).astype(bf16)
        turned = mul(kvt[...], cat[:, :LANES])
        stacked[g, pl.ds(start, LANES), :] = turned.T
        return carry

    def gather_heads(upper):
        first = HEAD_DIM if upper else 0
        lanes = slice(first, first + HEAD_DIM)
        for g in range(LOCAL):
            for h in range(0, SHARED, 2):
                left = stacked[g, h * both : (h + 1) * both, lanes]
                right = stacked[g, (h + 1) * both : (h + 2) * both, lanes]
                at = (g * SHARED + h) * HEAD_DIM
                halves[:, at : at + LANES] = jnp.concatenate([left, right], axis=1).astype(bf16)

    gr_copies = []
    for g in range(LOCAL):
        kv_arrived(kvb, 0, g)
        kvt[...] = kvb[g].astype(f32).T.astype(bf16)
        acc[g] = jnp.zeros((total, LANES), f32)
        lax.fori_loop(0, stack // LANES, functools.partial(backward_chunk, g), 0)
        gsend[g] = acc[g].astype(bf16)
        for k in range(1, GROUP):
            to = lax.rem(member + k, GROUP)
            copy = remote(
                gsend.at[g, pl.ds(to * rows, rows)], grecv.at[k, g],
                gr_send.at[g, k], gr_recv.at[g, k], {"ctx": base + to},
            )
            copy.start()
            gr_copies.append(copy)
    gather_heads(False)
    gq_send[...] = halves[theirs, :]
    pair_copies.append(pair_copy(3, gq_send, gq_all.at[core]))
    gq_all[core] = halves[mine, :]

    for g in range(LOCAL):
        kv_arrived(kvf, 1, g)
        kvt[...] = kvf[g].astype(f32).T.astype(bf16)
        lax.fori_loop(0, stack // LANES, functools.partial(forward_chunk, g), 0)
    gather_heads(True)
    mix_send[...] = halves[theirs, :]
    pair_copies.append(pair_copy(4, mix_send, mix_all.at[core]))
    mix_all[core] = halves[mine, :]
    pair_arrived(4, mix_all.at[other])
    made = xf[mine, :].astype(f32)
    for p in range(PAIR):
        made += mul(mix_all[p], wo[p * half : (p + 1) * half, :])
    of[...] = made.astype(bf16)

    def shift(at, src, dst, where, edge, arrive_edge):
        small = remote(
            src.at[pl.ds(0, mem)], dst.at[pl.ds(0, mem)],
            sec_send.at[at, 0], sec_recv.at[at, 0], {"section": where},
        )
        large = remote(
            src.at[pl.ds(mem, tokens)], dst.at[pl.ds(mem, tokens)],
            sec_send.at[at, 1], sec_recv.at[at, 1], {"section": where},
        )
        small.start()

        @pl.when(section != edge)
        def _():
            large.start()

        def finish():
            small.wait()

            @pl.when(section != edge)
            def _():
                large.wait_send()

            @pl.when(section != arrive_edge)
            def _():
                large.wait_recv()

        return finish

    finish_f = shift(0, of, outf_h, after, sections - 1, 0)

    for g in range(LOCAL):
        own = acc[g, pl.ds(member * rows, rows), :]
        cross = None
        for k in range(1, GROUP):
            source = lax.rem(member + GROUP - k, GROUP)
            place = grecv.at[k, g]
            remote(
                place, place, gr_send.at[g, k], gr_recv.at[g, k], {"ctx": base + source}
            ).wait_recv()
            value = grecv[k, g].astype(f32)
            if k % PAIR == 0:
                own = own + value
            else:
                cross = value if cross is None else cross + value
        gsum[core * LOCAL + g] = own
        gsum[other * LOCAL + g] = cross
    pair_arrived(3, gq_all.at[other])
    parts = [gsum[h, :, :HEAD_DIM] for h in range(KV_HEADS)]
    parts += [gsum[h, :, HEAD_DIM:] for h in range(KV_HEADS)]
    grad_kv = jnp.concatenate(parts, axis=1).astype(bf16)
    grad_normed = mul(grad_kv, wkv[...], NT)
    for p in range(PAIR):
        grad_normed += mul(gq_all[p], wq[:, p * half : (p + 1) * half], NT)
    values, scale = norm(xb[mine, :])
    plain = values * scale
    pushed = gain * grad_normed
    grad_in = cot[mine, :].astype(f32) + scale * (
        pushed - plain * jnp.mean(pushed * plain, axis=-1, keepdims=True)
    )
    ob[...] = grad_in.astype(bf16)
    finish_b = shift(1, ob, outb_h, before, 0, sections - 1)

    for copy in pair_copies + kv_copies + gr_copies:
        copy.wait_send()
    finish_f()
    finish_b()


def shards(fwd_in, bwd_saved, bwd_cot, new_tokens, loss_cot, gain, w_query, w_keyval, w_out):
    section_now = lax.axis_index("section")
    sections = lax.axis_size("section")
    rows, width = fwd_in.shape[1:]
    mem = rows - new_tokens.shape[0]
    both = PAIR * rows
    total = GROUP * rows
    stack = SHARED * both
    half = width // PAIR
    anywhere = pl.BlockSpec(memory_space=pl.ANY)
    block = jax.ShapeDtypeStruct((rows, width), bf16)
    vmem = pltpu.VMEM
    dma = pltpu.SemaphoreType.DMA
    arrived, returned = pl.pallas_call(
        functools.partial(kernel, sections, mem),
        out_shape=(block, block),
        in_specs=[anywhere] * 3 + [pl.BlockSpec(memory_space=pltpu.VMEM)] + [anywhere] * 3,
        out_specs=(anywhere, anywhere),
        scratch_shapes=[
            vmem((both, width), bf16), vmem((both, width), bf16), vmem((both, width), bf16),
            vmem(w_query.shape[1:], bf16), vmem(w_keyval.shape[1:], bf16), vmem(w_out.shape[1:], bf16),
            vmem((both, width), bf16),
            vmem((LOCAL, total, LANES), bf16), vmem((LOCAL, total, LANES), bf16),
            vmem((LANES, total), bf16),
            vmem((LOCAL, stack, LANES), bf16), vmem((LOCAL, stack, LANES), bf16),
            vmem((LOCAL, stack, LANES), bf16),
            vmem((total, LANES), jnp.int32),
            vmem((total, 2 * LANES), f32), vmem((total, LANES), f32), vmem((total, 2 * LANES), bf16),
            vmem((LOCAL, total, LANES), f32), vmem((LOCAL, total, LANES), bf16),
            vmem((GROUP, LOCAL, rows, LANES), bf16), vmem((KV_HEADS, rows, LANES), f32),
            vmem((LOCAL, stack, LANES), f32), vmem((both, half), bf16),
            vmem((rows, half), bf16), vmem((PAIR, rows, half), bf16),
            vmem((rows, half), bf16), vmem((PAIR, rows, half), bf16),
            vmem((rows, width), bf16), vmem((rows, width), bf16),
            dma((6,)), dma((5,)), dma((5,)),
            dma((2, LOCAL, CHIPS)), dma((2, LOCAL, CHIPS)),
            dma((LOCAL, GROUP)), dma((LOCAL, GROUP)),
            dma((2, 2)), dma((2, 2)),
        ],
        compiler_params=pltpu.CompilerParams(
            collective_id=0, has_side_effects=True, vmem_limit_bytes=60 * 1024 * 1024
        ),
    )(fwd_in[0], bwd_saved[0], bwd_cot[0], gain, w_query[0], w_keyval[0], w_out[0])
    head_rows = jnp.concatenate([arrived[:mem], new_tokens], axis=0)
    fwd_next = jnp.where(section_now == 0, head_rows, arrived)[None]
    tail_rows = jnp.concatenate([returned[:mem], loss_cot], axis=0)
    cot_next = jnp.where(section_now == sections - 1, tail_rows, returned)[None]
    return (fwd_next, cot_next)


def solution(mesh):
    return jax.shard_map(
        shards,
        mesh=mesh,
        in_specs=(
            P("section", "ctx", None),
            P("section", "ctx", None),
            P("section", "ctx", None),
            P("ctx", None),
            P("ctx", None),
            P("section", None),
            P("section", None, None),
            P("section", None, None),
            P("section", None, None),
        ),
        out_specs=(P("section", "ctx", None), P("section", "ctx", None)),
        check_vma=False,
    )
```

```python
import functools

import jax
import jax.numpy as jnp
from jax import lax
from jax.experimental import pallas as pl
from jax.experimental.pallas import tpu as pltpu
from jax.sharding import PartitionSpec as P

HEADS = 16
KV_HEADS = 4
HEAD_DIM = 64
GROUP = 8
PAIR = 2
CHIPS = GROUP // PAIR
LOCAL = KV_HEADS // PAIR
SHARED = HEADS // KV_HEADS
LANES = 128
PIECES = 4

epsilon = 1e-05
far = 1 << 30

bf16 = jnp.bfloat16
f32 = jnp.float32
NT = (((1,), (1,)), ((), ()))
NN = (((1,), (0,)), ((), ()))


def mul(a, b, dims=NN):
    return lax.dot_general(a, b, dims, preferred_element_type=f32)


def kernel(
    sections, mem,
    xf_h, xb_h, cot_h, gain_ref, wq_h, wkv_h, wo_h,
    outf_h, outb_h,
    xf, xb, cot, wq, wkv, wo, normed, kvf, kvb, kvt, qf, qb, gb, kpos,
    sd, ex, cat, acc, gsend, grecv, gpass, gsum, kvown, stacked, halves, gq_send, gq_all, mix_send, mix_all,
    of, ob,
    local_sem, pair_send, pair_recv, kv_send, kv_recv, gr_send, gr_recv, sec_send, sec_recv,
    hop_send, hop_recv,
):
    rows = xf_h.shape[0]
    width = xf_h.shape[1]
    both = PAIR * rows
    total = GROUP * rows
    stack = SHARED * both
    half = width // PAIR
    tokens = rows - mem

    ctx = lax.axis_index("ctx")
    section = lax.axis_index("section")
    member = lax.rem(ctx, GROUP)
    base = ctx - member
    core = lax.rem(member, PAIR)
    chip = member // PAIR
    other = 1 - core
    partner = base + chip * PAIR + other

    loads = []
    mine = pl.ds(core * rows, rows)
    for at, (src, dst) in enumerate(
        [
            (xb_h, xb.at[mine]), (wkv_h, wkv), (xf_h, xf.at[mine]),
            (wq_h, wq), (cot_h, cot.at[mine]), (wo_h, wo),
        ]
    ):
        copy = pltpu.make_async_copy(src, dst, local_sem.at[at])
        copy.start()
        loads.append(copy)
    load_xb, load_wkv, load_xf, load_wq, load_cot, load_wo = loads

    after = lax.rem(section + 1, sections)
    before = lax.rem(section + sections - 1, sections)
    barrier = pltpu.get_barrier_semaphore()
    for k in range(1, GROUP):
        pl.semaphore_signal(
            barrier, inc=1, device_id={"ctx": base + lax.rem(member + k, GROUP)},
            device_id_type=pl.DeviceIdType.MESH,
        )
    for neighbour in (after, before):
        pl.semaphore_signal(
            barrier, inc=1, device_id={"section": neighbour},
            device_id_type=pl.DeviceIdType.MESH,
        )
    pl.semaphore_wait(barrier, GROUP + 1)

    def remote(src, dst, send, recv, where):
        return pltpu.make_async_remote_copy(
            src_ref=src, dst_ref=dst, send_sem=send, recv_sem=recv,
            device_id=where, device_id_type=pl.DeviceIdType.MESH,
        )

    theirs = pl.ds(other * rows, rows)

    def pair_copy(at, src, dst):
        copy = remote(src, dst, pair_send.at[at], pair_recv.at[at], {"ctx": partner})
        copy.start()
        return copy

    pair_copies = [
        pair_copy(0, xb_h, xb.at[mine]),
        pair_copy(1, xf_h, xf.at[mine]),
        pair_copy(2, cot_h, cot.at[mine]),
    ]

    def pair_arrived(at, dst):
        remote(dst, dst, pair_send.at[at], pair_recv.at[at], {"ctx": partner}).wait_recv()

    for b in range(GROUP):
        inner = lax.broadcasted_iota(jnp.int32, (rows, LANES), 0)
        kpos[b * rows : (b + 1) * rows, :] = jnp.where(
            inner < mem, -1, b * tokens + inner - mem
        )

    gain = gain_ref[...].astype(f32)

    def norm(x):
        values = x.astype(f32)
        scale = lax.rsqrt(jnp.mean(values * values, axis=-1, keepdims=True) + epsilon)
        return values, scale

    def make_normed(x_ref, place):
        values, scale = norm(x_ref[place, :])
        normed[place, :] = (values * scale * gain).astype(bf16)

    last = CHIPS - 1
    is_end = jnp.logical_or(chip == 0, chip == last)
    is_middle = jnp.logical_not(is_end)
    opposite = last - chip
    hop_from = jnp.where(chip == 1, last, 0)
    hop_to = last - hop_from
    sum_via = jnp.where(chip == 0, 1, last - 1)
    sum_from = jnp.where(chip == 1, 0, last)

    def peer(k):
        return lax.rem(member + k, GROUP)

    def source(k):
        return lax.rem(member + GROUP - k, GROUP)

    def is_far(one):
        return jnp.logical_and(is_end, one // PAIR == opposite)

    order = sorted(range(1, GROUP), key=lambda k: abs(k - GROUP // 2))

    def project_kv(kv_ref, kind):
        keyval = mul(normed[mine, :], wkv[...])
        for h in range(KV_HEADS):
            at = h * HEAD_DIM
            after_keys = KV_HEADS * HEAD_DIM + at
            kvown[kind, h] = jnp.concatenate(
                [keyval[:, at : at + HEAD_DIM], keyval[:, after_keys : after_keys + HEAD_DIM]],
                axis=1,
            ).astype(bf16)
        for g in range(LOCAL):
            kv_ref[g, pl.ds(member * rows, rows), :] = kvown[kind, core * LOCAL + g]

    def kv_copy(kv_ref, kind, g, k):
        to = peer(k)
        return remote(
            kvown.at[kind, lax.rem(to, PAIR) * LOCAL + g],
            kv_ref.at[g, pl.ds(member * rows, rows)],
            kv_send.at[kind, g, k], kv_recv.at[kind, g, k], {"ctx": base + to},
        )

    def send_kv(kv_ref, kind):
        for g in range(LOCAL):
            for k in order:
                @pl.when(jnp.logical_not(is_far(peer(k))))
                def _():
                    kv_copy(kv_ref, kind, g, k).start()

    def finish_kv(kv_ref, kind):
        for g in range(LOCAL):
            for k in order:
                @pl.when(jnp.logical_not(is_far(peer(k))))
                def _():
                    kv_copy(kv_ref, kind, g, k).wait_send()

            @pl.when(is_middle)
            def _():
                hop_copy(kv_ref, kind, g).wait_send()

    def hop_copy(kv_ref, kind, g):
        place = kv_ref.at[g, pl.ds(hop_from * both, both)]
        return remote(
            place, place, hop_send.at[kind, g], hop_recv.at[kind, g],
            {"ctx": base + hop_to * PAIR + core},
        )

    def kv_wait(kv_ref, kind, g, one):
        k = lax.rem(member + GROUP - one, GROUP)
        place = kv_ref.at[g, pl.ds(one * rows, rows)]
        remote(
            place, place, kv_send.at[kind, g, k], kv_recv.at[kind, g, k], {"ctx": base + one}
        ).wait_recv()

    def hop_kv(kv_ref, kind, g):
        @pl.when(is_middle)
        def _():
            for c in range(PAIR):
                kv_wait(kv_ref, kind, g, hop_from * PAIR + c)
            hop_copy(kv_ref, kind, g).start()

    def kv_arrived(kv_ref, kind, g):
        for k in range(1, GROUP):
            one = source(k)
            done = jnp.logical_and(is_middle, one // PAIR == hop_from)

            @pl.when(jnp.logical_not(jnp.logical_or(is_far(one), done)))
            def _():
                kv_wait(kv_ref, kind, g, one)

        @pl.when(is_end)
        def _():
            place = kv_ref.at[g, pl.ds(opposite * both, both)]
            remote(
                place, place, hop_send.at[kind, g], hop_recv.at[kind, g],
                {"ctx": base + opposite * PAIR + core},
            ).wait_recv()

    def gr_copy(g, k):
        to = peer(k)
        return remote(
            gsend.at[g, pl.ds(to * rows, rows)], grecv.at[k, g],
            gr_send.at[g, k], gr_recv.at[g, k], {"ctx": base + to},
        )

    def is_summed(one):
        return jnp.logical_and(is_middle, one // PAIR == last - sum_from)

    def sum_copy(g, where):
        return remote(
            gsend.at[g, pl.ds(opposite * both, both)], gpass.at[g],
            hop_send.at[2, g], hop_recv.at[2, g], {"ctx": base + where * PAIR + core},
        )

    def send_sums(g):
        gsend[g] = acc[g].astype(bf16)

        @pl.when(is_end)
        def _():
            sum_copy(g, sum_via).start()

        for k in order:
            to = peer(k)

            @pl.when(jnp.logical_not(jnp.logical_or(is_far(to), is_summed(to))))
            def _():
                gr_copy(g, k).start()

    def hop_sums(g):
        @pl.when(is_middle)
        def _():
            sum_copy(g, sum_from).wait_recv()
            place = pl.ds((last - sum_from) * both, both)
            gsend[g, place, :] = (acc[g, place, :] + gpass[g].astype(f32)).astype(bf16)
            for k in order:
                @pl.when(is_summed(peer(k)))
                def _():
                    gr_copy(g, k).start()

    def finish_sums(g):
        @pl.when(is_end)
        def _():
            sum_copy(g, sum_via).wait_send()

        for k in order:
            @pl.when(jnp.logical_not(is_far(peer(k))))
            def _():
                gr_copy(g, k).wait_send()

    def spread(matrix, dst, upper, factor):
        rounded = matrix.astype(bf16).astype(f32) * factor
        zero = jnp.zeros((both, HEAD_DIM), f32)
        for g in range(LOCAL):
            for h in range(SHARED):
                at = (g * SHARED + h) * HEAD_DIM
                piece = rounded[:, at : at + HEAD_DIM]
                parts = [zero, piece] if upper else [piece, zero]
                dst[g, h * both : (h + 1) * both, :] = jnp.concatenate(parts, axis=1).astype(bf16)

    scale_by = HEAD_DIM ** (-0.5)
    my_cols = pl.ds(pl.multiple_of(core * half, half), half)

    load_xb.wait()
    make_normed(xb, mine)
    load_wkv.wait()
    project_kv(kvb, 0)
    send_kv(kvb, 0)
    pair_arrived(0, xb.at[theirs])
    make_normed(xb, theirs)
    load_wq.wait()
    spread(mul(normed[...], wq[:, my_cols]), qb, False, scale_by)
    load_cot.wait()
    pair_arrived(2, cot.at[theirs])
    load_wo.wait()
    spread(mul(cot[...], wo[my_cols, :], NT), gb, True, 1.0)
    load_xf.wait()
    make_normed(xf, mine)
    project_kv(kvf, 1)
    hop_kv(kvb, 0, 0)
    pair_arrived(1, xf.at[theirs])
    make_normed(xf, theirs)
    spread(mul(normed[...], wq[:, my_cols]), qf, False, scale_by)

    step = total // PIECES

    def query_positions(start):
        row = start + lax.broadcasted_iota(jnp.int32, (1, LANES), 1)
        for h in range(1, SHARED):
            row = jnp.where(row >= both, row - both, row)
        block = jnp.where(row >= rows, 1, 0)
        inner = row - block * rows
        return jnp.where(inner < mem, far, (chip * PAIR + block) * tokens + inner - mem)

    def backward_chunk(g, i, carry):
        start = pl.multiple_of(i * LANES, LANES)
        pair = jnp.concatenate([qb[g, pl.ds(start, LANES), :], gb[g, pl.ds(start, LANES), :]], axis=0)
        position = query_positions(start)
        top = None
        for p in range(PIECES):
            part = slice(p * step, (p + 1) * step)
            product = mul(kvb[g, part, :], pair, NT)
            scores = jnp.where(kpos[part, :] <= position, product[:, :LANES], -1e30)
            sd[part, :LANES] = scores
            sd[part, LANES:] = product[:, LANES:]
            peak = jnp.max(scores, axis=0, keepdims=True)
            top = peak if top is None else jnp.maximum(top, peak)
        norm_sum = jnp.zeros((1, LANES), f32)
        delta = jnp.zeros((1, LANES), f32)
        for p in range(PIECES):
            part = slice(p * step, (p + 1) * step)
            expd = jnp.exp(sd[part, :LANES] - top)
            ex[part, :] = expd
            norm_sum += jnp.sum(expd, axis=0, keepdims=True)
            delta += jnp.sum(expd * sd[part, LANES:], axis=0, keepdims=True)
        inverse = 1.0 / norm_sum
        delta = delta * inverse
        for p in range(PIECES):
            part = slice(p * step, (p + 1) * step)
            probs = ex[part, :] * inverse
            cat[part, LANES:] = probs.astype(bf16)
            cat[part, :LANES] = (probs * (sd[part, LANES:] - delta)).astype(bf16)
            acc[g, part, :] += mul(cat[part, :], pair)
        turned = mul(kvt[...], cat[:, :LANES])
        stacked[g, pl.ds(start, LANES), :] = turned.T * scale_by
        return carry

    def forward_chunk(g, i, carry):
        start = pl.multiple_of(i * LANES, LANES)
        queries = qf[g, pl.ds(start, LANES), :]
        position = query_positions(start)
        top = None
        for p in range(PIECES):
            part = slice(p * step, (p + 1) * step)
            product = mul(kvf[g, part, :], queries, NT)
            scores = jnp.where(kpos[part, :] <= position, product, -1e30)
            sd[part, :LANES] = scores
            peak = jnp.max(scores, axis=0, keepdims=True)
            top = peak if top is None else jnp.maximum(top, peak)
        norm_sum = jnp.zeros((1, LANES), f32)
        for p in range(PIECES):
            part = slice(p * step, (p + 1) * step)
            expd = jnp.exp(sd[part, :LANES] - top)
            ex[part, :] = expd
            norm_sum += jnp.sum(expd, axis=0, keepdims=True)
        inverse = 1.0 / norm_sum
        for p in range(PIECES):
            part = slice(p * step, (p + 1) * step)
            cat[part, :LANES] = (ex[part, :] * inverse).astype(bf16)
        turned = mul(kvt[...], cat[:, :LANES])
        stacked[g, pl.ds(start, LANES), :] = turned.T
        return carry

    def gather_heads(upper):
        first = HEAD_DIM if upper else 0
        lanes = slice(first, first + HEAD_DIM)
        for g in range(LOCAL):
            for h in range(0, SHARED, 2):
                left = stacked[g, h * both : (h + 1) * both, lanes]
                right = stacked[g, (h + 1) * both : (h + 2) * both, lanes]
                at = (g * SHARED + h) * HEAD_DIM
                halves[:, at : at + LANES] = jnp.concatenate([left, right], axis=1).astype(bf16)

    def run(chunk, g, actions):
        def body(i, carry):
            for at, action in actions.items():
                pl.when(i == at)(action)
            return chunk(g, i, carry)

        lax.fori_loop(0, stack // LANES, body, 0)

    def go_on():
        hop_kv(kvb, 0, 1)
        send_kv(kvf, 1)

    backward_actions = [
        {2: go_on},
        {1: lambda: hop_kv(kvf, 1, 0), 4: lambda: hop_sums(0), 7: lambda: hop_kv(kvf, 1, 1)},
    ]
    for g in range(LOCAL):
        kv_arrived(kvb, 0, g)
        kvt[...] = kvb[g].astype(f32).T.astype(bf16)
        acc[g] = jnp.zeros((total, LANES), f32)
        run(backward_chunk, g, backward_actions[g])
        send_sums(g)
    gather_heads(False)
    gq_send[...] = halves[theirs, :]
    pair_copies.append(pair_copy(3, gq_send, gq_all.at[core]))
    gq_all[core] = halves[mine, :]

    for g in range(LOCAL):
        kv_arrived(kvf, 1, g)
        kvt[...] = kvf[g].astype(f32).T.astype(bf16)
        run(forward_chunk, g, {3: lambda: hop_sums(1)} if g == 0 else {})
    gather_heads(True)
    mix_send[...] = halves[theirs, :]
    pair_copies.append(pair_copy(4, mix_send, mix_all.at[core]))
    mix_all[core] = halves[mine, :]
    pair_arrived(4, mix_all.at[other])
    made = xf[mine, :].astype(f32)
    for p in range(PAIR):
        made += mul(mix_all[p], wo[p * half : (p + 1) * half, :])
    of[...] = made.astype(bf16)

    def shift(at, src, dst, where, edge, arrive_edge):
        small = remote(
            src.at[pl.ds(0, mem)], dst.at[pl.ds(0, mem)],
            sec_send.at[at, 0], sec_recv.at[at, 0], {"section": where},
        )
        large = remote(
            src.at[pl.ds(mem, tokens)], dst.at[pl.ds(mem, tokens)],
            sec_send.at[at, 1], sec_recv.at[at, 1], {"section": where},
        )
        small.start()

        @pl.when(section != edge)
        def _():
            large.start()

        def finish():
            small.wait()

            @pl.when(section != edge)
            def _():
                large.wait_send()

            @pl.when(section != arrive_edge)
            def _():
                large.wait_recv()

        return finish

    finish_f = shift(0, of, outf_h, after, sections - 1, 0)

    for g in range(LOCAL):
        own = acc[g, pl.ds(member * rows, rows), :]
        cross = None
        for k in range(1, GROUP):
            one = source(k)

            @pl.when(is_far(one))
            def _():
                grecv[k, g] = jnp.zeros((rows, LANES), bf16)

            @pl.when(jnp.logical_not(is_far(one)))
            def _():
                place = grecv.at[k, g]
                remote(
                    place, place, gr_send.at[g, k], gr_recv.at[g, k], {"ctx": base + one}
                ).wait_recv()

            value = grecv[k, g].astype(f32)
            if k % PAIR == 0:
                own = own + value
            else:
                cross = value if cross is None else cross + value
        gsum[core * LOCAL + g] = own
        gsum[other * LOCAL + g] = cross
    pair_arrived(3, gq_all.at[other])
    parts = [gsum[h, :, :HEAD_DIM] for h in range(KV_HEADS)]
    parts += [gsum[h, :, HEAD_DIM:] for h in range(KV_HEADS)]
    grad_kv = jnp.concatenate(parts, axis=1).astype(bf16)
    grad_normed = mul(grad_kv, wkv[...], NT)
    for p in range(PAIR):
        grad_normed += mul(gq_all[p], wq[:, p * half : (p + 1) * half], NT)
    values, scale = norm(xb[mine, :])
    plain = values * scale
    pushed = gain * grad_normed
    grad_in = cot[mine, :].astype(f32) + scale * (
        pushed - plain * jnp.mean(pushed * plain, axis=-1, keepdims=True)
    )
    ob[...] = grad_in.astype(bf16)
    finish_b = shift(1, ob, outb_h, before, 0, sections - 1)

    for copy in pair_copies:
        copy.wait_send()
    finish_kv(kvb, 0)
    finish_kv(kvf, 1)
    for g in range(LOCAL):
        finish_sums(g)
    finish_f()
    finish_b()


def shards(fwd_in, bwd_saved, bwd_cot, new_tokens, loss_cot, gain, w_query, w_keyval, w_out):
    section_now = lax.axis_index("section")
    sections = lax.axis_size("section")
    rows, width = fwd_in.shape[1:]
    mem = rows - new_tokens.shape[0]
    both = PAIR * rows
    total = GROUP * rows
    stack = SHARED * both
    half = width // PAIR
    anywhere = pl.BlockSpec(memory_space=pl.ANY)
    block = jax.ShapeDtypeStruct((rows, width), bf16)
    vmem = pltpu.VMEM
    dma = pltpu.SemaphoreType.DMA
    arrived, returned = pl.pallas_call(
        functools.partial(kernel, sections, mem),
        out_shape=(block, block),
        in_specs=[anywhere] * 3 + [pl.BlockSpec(memory_space=pltpu.VMEM)] + [anywhere] * 3,
        out_specs=(anywhere, anywhere),
        scratch_shapes=[
            vmem((both, width), bf16), vmem((both, width), bf16), vmem((both, width), bf16),
            vmem(w_query.shape[1:], bf16), vmem(w_keyval.shape[1:], bf16), vmem(w_out.shape[1:], bf16),
            vmem((both, width), bf16),
            vmem((LOCAL, total, LANES), bf16), vmem((LOCAL, total, LANES), bf16),
            vmem((LANES, total), bf16),
            vmem((LOCAL, stack, LANES), bf16), vmem((LOCAL, stack, LANES), bf16),
            vmem((LOCAL, stack, LANES), bf16),
            vmem((total, LANES), jnp.int32),
            vmem((total, 2 * LANES), f32), vmem((total, LANES), f32), vmem((total, 2 * LANES), bf16),
            vmem((LOCAL, total, LANES), f32), vmem((LOCAL, total, LANES), bf16),
            vmem((GROUP, LOCAL, rows, LANES), bf16), vmem((LOCAL, both, LANES), bf16),
            vmem((KV_HEADS, rows, LANES), f32), vmem((2, KV_HEADS, rows, LANES), bf16),
            vmem((LOCAL, stack, LANES), f32), vmem((both, half), bf16),
            vmem((rows, half), bf16), vmem((PAIR, rows, half), bf16),
            vmem((rows, half), bf16), vmem((PAIR, rows, half), bf16),
            vmem((rows, width), bf16), vmem((rows, width), bf16),
            dma((6,)), dma((5,)), dma((5,)),
            dma((2, LOCAL, GROUP)), dma((2, LOCAL, GROUP)),
            dma((LOCAL, GROUP)), dma((LOCAL, GROUP)),
            dma((2, 2)), dma((2, 2)),
            dma((3, LOCAL)), dma((3, LOCAL)),
        ],
        compiler_params=pltpu.CompilerParams(
            collective_id=0, has_side_effects=True, vmem_limit_bytes=60 * 1024 * 1024
        ),
    )(fwd_in[0], bwd_saved[0], bwd_cot[0], gain, w_query[0], w_keyval[0], w_out[0])
    token_row = lax.broadcasted_iota(jnp.int32, (rows, 1), 0) >= mem
    edge = jnp.pad(new_tokens, ((mem, 0), (0, 0)))
    fwd_next = jnp.where(token_row & (section_now == 0), edge, arrived)[None]
    edge = jnp.pad(loss_cot, ((mem, 0), (0, 0)))
    cot_next = jnp.where(token_row & (section_now == sections - 1), edge, returned)[None]
    return (fwd_next, cot_next)


def solution(mesh):
    return jax.shard_map(
        shards,
        mesh=mesh,
        in_specs=(
            P("section", "ctx", None),
            P("section", "ctx", None),
            P("section", "ctx", None),
            P("ctx", None),
            P("ctx", None),
            P("section", None),
            P("section", None, None),
            P("section", None, None),
            P("section", None, None),
        ),
        out_specs=(P("section", "ctx", None), P("section", "ctx", None)),
        check_vma=False,
    )
```

```python
import functools

import jax
import jax.numpy as jnp
from jax import lax
from jax.experimental import pallas as pl
from jax.experimental.pallas import tpu as pltpu
from jax.sharding import PartitionSpec as P

HEADS = 16
KV_HEADS = 4
HEAD_DIM = 64
GROUP = 8
PAIR = 2
CHIPS = GROUP // PAIR
LOCAL = KV_HEADS // PAIR
SHARED = HEADS // KV_HEADS
LANES = 128
PIECES = 4
UNROLL = 3

epsilon = 1e-05
far = 1 << 30

bf16 = jnp.bfloat16
f32 = jnp.float32
NT = (((1,), (1,)), ((), ()))
NN = (((1,), (0,)), ((), ()))


def mul(a, b, dims=NN):
    return lax.dot_general(a, b, dims, preferred_element_type=f32)


def kernel(
    sections, mem,
    xf_h, xb_h, cot_h, gain_ref, wq_h, wkv_h, wo_h,
    outf_h, outb_h,
    xf, xb, cot, wq, wkv, wo, normed, kvf, kvb, kvt, qf, qb, gb, kpos,
    sd, ex, cat, acc, gsend, grecv, gpass, gsum, kvown, stacked, halves, gq_send, gq_all, mix_send, mix_all,
    of, ob,
    local_sem, pair_send, pair_recv, kv_send, kv_recv, gr_send, gr_recv, sec_send, sec_recv,
    hop_send, hop_recv,
):
    rows = xf_h.shape[0]
    width = xf_h.shape[1]
    both = PAIR * rows
    total = GROUP * rows
    stack = SHARED * both
    half = width // PAIR
    tokens = rows - mem

    ctx = lax.axis_index("ctx")
    section = lax.axis_index("section")
    member = lax.rem(ctx, GROUP)
    base = ctx - member
    core = lax.rem(member, PAIR)
    chip = member // PAIR
    other = 1 - core
    partner = base + chip * PAIR + other

    loads = []
    mine = pl.ds(core * rows, rows)
    for at, (src, dst) in enumerate(
        [
            (xb_h, xb.at[mine]), (wkv_h, wkv), (xf_h, xf.at[mine]),
            (wq_h, wq), (cot_h, cot.at[mine]), (wo_h, wo),
        ]
    ):
        copy = pltpu.make_async_copy(src, dst, local_sem.at[at])
        copy.start()
        loads.append(copy)
    load_xb, load_wkv, load_xf, load_wq, load_cot, load_wo = loads

    after = lax.rem(section + 1, sections)
    before = lax.rem(section + sections - 1, sections)
    barrier = pltpu.get_barrier_semaphore()
    for k in range(1, GROUP):
        pl.semaphore_signal(
            barrier, inc=1, device_id={"ctx": base + lax.rem(member + k, GROUP)},
            device_id_type=pl.DeviceIdType.MESH,
        )
    for neighbour in (after, before):
        pl.semaphore_signal(
            barrier, inc=1, device_id={"section": neighbour},
            device_id_type=pl.DeviceIdType.MESH,
        )
    pl.semaphore_wait(barrier, GROUP + 1)

    def remote(src, dst, send, recv, where):
        return pltpu.make_async_remote_copy(
            src_ref=src, dst_ref=dst, send_sem=send, recv_sem=recv,
            device_id=where, device_id_type=pl.DeviceIdType.MESH,
        )

    theirs = pl.ds(other * rows, rows)

    def pair_copy(at, src, dst):
        copy = remote(src, dst, pair_send.at[at], pair_recv.at[at], {"ctx": partner})
        copy.start()
        return copy

    pair_copies = [
        pair_copy(0, xb_h, xb.at[mine]),
        pair_copy(1, xf_h, xf.at[mine]),
        pair_copy(2, cot_h, cot.at[mine]),
    ]

    def pair_arrived(at, dst):
        remote(dst, dst, pair_send.at[at], pair_recv.at[at], {"ctx": partner}).wait_recv()

    for b in range(GROUP):
        inner = lax.broadcasted_iota(jnp.int32, (rows, LANES), 0)
        kpos[b * rows : (b + 1) * rows, :] = jnp.where(
            inner < mem, -1, b * tokens + inner - mem
        )

    gain = gain_ref[...].astype(f32)

    def norm(x):
        values = x.astype(f32)
        scale = lax.rsqrt(jnp.mean(values * values, axis=-1, keepdims=True) + epsilon)
        return values, scale

    def make_normed(x_ref, place):
        values, scale = norm(x_ref[place, :])
        normed[place, :] = (values * scale * gain).astype(bf16)

    last = CHIPS - 1
    is_end = jnp.logical_or(chip == 0, chip == last)
    is_middle = jnp.logical_not(is_end)
    opposite = last - chip
    hop_from = jnp.where(chip == 1, last, 0)
    hop_to = last - hop_from
    sum_via = jnp.where(chip == 0, 1, last - 1)
    sum_from = jnp.where(chip == 1, 0, last)

    def peer(k):
        return lax.rem(member + k, GROUP)

    def source(k):
        return lax.rem(member + GROUP - k, GROUP)

    def is_far(one):
        return jnp.logical_and(is_end, one // PAIR == opposite)

    order = sorted(range(1, GROUP), key=lambda k: abs(k - GROUP // 2))

    def project_kv(kv_ref, kind):
        keyval = mul(normed[mine, :], wkv[...])
        for h in range(KV_HEADS):
            at = h * HEAD_DIM
            after_keys = KV_HEADS * HEAD_DIM + at
            kvown[kind, h] = jnp.concatenate(
                [keyval[:, at : at + HEAD_DIM], keyval[:, after_keys : after_keys + HEAD_DIM]],
                axis=1,
            ).astype(bf16)
        for g in range(LOCAL):
            kv_ref[g, pl.ds(member * rows, rows), :] = kvown[kind, core * LOCAL + g]

    def kv_copy(kv_ref, kind, g, k):
        to = peer(k)
        return remote(
            kvown.at[kind, lax.rem(to, PAIR) * LOCAL + g],
            kv_ref.at[g, pl.ds(member * rows, rows)],
            kv_send.at[kind, g, k], kv_recv.at[kind, g, k], {"ctx": base + to},
        )

    def send_kv(kv_ref, kind):
        for g in range(LOCAL):
            for k in order:
                @pl.when(jnp.logical_not(is_far(peer(k))))
                def _():
                    kv_copy(kv_ref, kind, g, k).start()

    def finish_kv(kv_ref, kind):
        for g in range(LOCAL):
            for k in order:
                @pl.when(jnp.logical_not(is_far(peer(k))))
                def _():
                    kv_copy(kv_ref, kind, g, k).wait_send()

            @pl.when(is_middle)
            def _():
                hop_copy(kv_ref, kind, g).wait_send()

    def hop_copy(kv_ref, kind, g):
        place = kv_ref.at[g, pl.ds(hop_from * both, both)]
        return remote(
            place, place, hop_send.at[kind, g], hop_recv.at[kind, g],
            {"ctx": base + hop_to * PAIR + core},
        )

    def kv_wait(kv_ref, kind, g, one):
        k = lax.rem(member + GROUP - one, GROUP)
        place = kv_ref.at[g, pl.ds(one * rows, rows)]
        remote(
            place, place, kv_send.at[kind, g, k], kv_recv.at[kind, g, k], {"ctx": base + one}
        ).wait_recv()

    def hop_kv(kv_ref, kind, g):
        @pl.when(is_middle)
        def _():
            for c in range(PAIR):
                kv_wait(kv_ref, kind, g, hop_from * PAIR + c)
            hop_copy(kv_ref, kind, g).start()

    def kv_arrived(kv_ref, kind, g):
        for k in range(1, GROUP):
            one = source(k)
            done = jnp.logical_and(is_middle, one // PAIR == hop_from)

            @pl.when(jnp.logical_not(jnp.logical_or(is_far(one), done)))
            def _():
                kv_wait(kv_ref, kind, g, one)

        @pl.when(is_end)
        def _():
            place = kv_ref.at[g, pl.ds(opposite * both, both)]
            remote(
                place, place, hop_send.at[kind, g], hop_recv.at[kind, g],
                {"ctx": base + opposite * PAIR + core},
            ).wait_recv()

    def gr_copy(g, k):
        to = peer(k)
        return remote(
            gsend.at[g, pl.ds(to * rows, rows)], grecv.at[k, g],
            gr_send.at[g, k], gr_recv.at[g, k], {"ctx": base + to},
        )

    def is_summed(one):
        return jnp.logical_and(is_middle, one // PAIR == last - sum_from)

    def sum_copy(g, where):
        return remote(
            gsend.at[g, pl.ds(opposite * both, both)], gpass.at[g],
            hop_send.at[2, g], hop_recv.at[2, g], {"ctx": base + where * PAIR + core},
        )

    def send_sums(g):
        gsend[g] = acc[g].astype(bf16)

        @pl.when(is_end)
        def _():
            sum_copy(g, sum_via).start()

        for k in order:
            to = peer(k)

            @pl.when(jnp.logical_not(jnp.logical_or(is_far(to), is_summed(to))))
            def _():
                gr_copy(g, k).start()

    def hop_sums(g):
        @pl.when(is_middle)
        def _():
            sum_copy(g, sum_from).wait_recv()
            place = pl.ds((last - sum_from) * both, both)
            gsend[g, place, :] = (acc[g, place, :] + gpass[g].astype(f32)).astype(bf16)
            for k in order:
                @pl.when(is_summed(peer(k)))
                def _():
                    gr_copy(g, k).start()

    def finish_sums(g):
        @pl.when(is_end)
        def _():
            sum_copy(g, sum_via).wait_send()

        for k in order:
            @pl.when(jnp.logical_not(is_far(peer(k))))
            def _():
                gr_copy(g, k).wait_send()

    def spread(matrix, dst, upper, factor):
        rounded = matrix.astype(bf16).astype(f32) * factor
        zero = jnp.zeros((both, HEAD_DIM), f32)
        for g in range(LOCAL):
            for h in range(SHARED):
                at = (g * SHARED + h) * HEAD_DIM
                piece = rounded[:, at : at + HEAD_DIM]
                parts = [zero, piece] if upper else [piece, zero]
                dst[g, h * both : (h + 1) * both, :] = jnp.concatenate(parts, axis=1).astype(bf16)

    scale_by = HEAD_DIM ** (-0.5)
    my_cols = pl.ds(pl.multiple_of(core * half, half), half)

    load_xb.wait()
    make_normed(xb, mine)
    load_wkv.wait()
    project_kv(kvb, 0)
    send_kv(kvb, 0)
    pair_arrived(0, xb.at[theirs])
    make_normed(xb, theirs)
    load_wq.wait()
    spread(mul(normed[...], wq[:, my_cols]), qb, False, scale_by)
    load_cot.wait()
    pair_arrived(2, cot.at[theirs])
    load_wo.wait()
    spread(mul(cot[...], wo[my_cols, :], NT), gb, True, 1.0)
    load_xf.wait()
    make_normed(xf, mine)
    project_kv(kvf, 1)
    hop_kv(kvb, 0, 0)
    pair_arrived(1, xf.at[theirs])
    make_normed(xf, theirs)
    spread(mul(normed[...], wq[:, my_cols]), qf, False, scale_by)

    step = total // PIECES

    def query_positions(start):
        row = start + lax.broadcasted_iota(jnp.int32, (1, LANES), 1)
        for h in range(1, SHARED):
            row = jnp.where(row >= both, row - both, row)
        block = jnp.where(row >= rows, 1, 0)
        inner = row - block * rows
        return jnp.where(inner < mem, far, (chip * PAIR + block) * tokens + inner - mem)

    parts = [slice(p * step, (p + 1) * step) for p in range(PIECES)]

    def backward_chunk(g, chunks):
        starts = [pl.multiple_of(i * LANES, LANES) for i in chunks]
        pairs = [
            jnp.concatenate([qb[g, pl.ds(at, LANES), :], gb[g, pl.ds(at, LANES), :]], axis=0)
            for at in starts
        ]
        for u, start in enumerate(starts):
            position = query_positions(start)
            top = None
            for part in parts:
                product = mul(kvb[g, part, :], pairs[u], NT)
                scores = jnp.where(kpos[part, :] <= position, product[:, :LANES], -1e30)
                sd[u, part, :LANES] = scores
                sd[u, part, LANES:] = product[:, LANES:]
                peak = jnp.max(scores, axis=0, keepdims=True)
                top = peak if top is None else jnp.maximum(top, peak)
            norm_sum = jnp.zeros((1, LANES), f32)
            delta = jnp.zeros((1, LANES), f32)
            for part in parts:
                expd = jnp.exp(sd[u, part, :LANES] - top)
                ex[u, part, :] = expd
                norm_sum += jnp.sum(expd, axis=0, keepdims=True)
                delta += jnp.sum(expd * sd[u, part, LANES:], axis=0, keepdims=True)
            inverse = 1.0 / norm_sum
            delta = delta * inverse
            at = u * 2 * LANES
            for part in parts:
                probs = ex[u, part, :] * inverse
                cat[part, at + LANES : at + 2 * LANES] = probs.astype(bf16)
                cat[part, at : at + LANES] = (probs * (sd[u, part, LANES:] - delta)).astype(bf16)
        everything = jnp.concatenate(pairs, axis=0)
        for part in parts:
            acc[g, part, :] += mul(cat[part, :], everything)
        for u, start in enumerate(starts):
            at = u * 2 * LANES
            turned = mul(kvt[...], cat[:, at : at + LANES])
            stacked[g, pl.ds(start, LANES), :] = turned.T * scale_by

    def forward_chunk(g, chunks):
        for u, i in enumerate(chunks):
            start = pl.multiple_of(i * LANES, LANES)
            queries = qf[g, pl.ds(start, LANES), :]
            position = query_positions(start)
            top = None
            for part in parts:
                product = mul(kvf[g, part, :], queries, NT)
                scores = jnp.where(kpos[part, :] <= position, product, -1e30)
                sd[u, part, :LANES] = scores
                peak = jnp.max(scores, axis=0, keepdims=True)
                top = peak if top is None else jnp.maximum(top, peak)
            norm_sum = jnp.zeros((1, LANES), f32)
            for part in parts:
                expd = jnp.exp(sd[u, part, :LANES] - top)
                ex[u, part, :] = expd
                norm_sum += jnp.sum(expd, axis=0, keepdims=True)
            inverse = 1.0 / norm_sum
            for part in parts:
                cat[part, u * LANES : (u + 1) * LANES] = (ex[u, part, :] * inverse).astype(bf16)
        turned = mul(kvt[...], cat[:, : len(chunks) * LANES])
        for u, i in enumerate(chunks):
            start = pl.multiple_of(i * LANES, LANES)
            stacked[g, pl.ds(start, LANES), :] = turned[:, u * LANES : (u + 1) * LANES].T

    def gather_heads(upper):
        first = HEAD_DIM if upper else 0
        lanes = slice(first, first + HEAD_DIM)
        for g in range(LOCAL):
            for h in range(0, SHARED, 2):
                left = stacked[g, h * both : (h + 1) * both, lanes]
                right = stacked[g, (h + 1) * both : (h + 2) * both, lanes]
                at = (g * SHARED + h) * HEAD_DIM
                halves[:, at : at + LANES] = jnp.concatenate([left, right], axis=1).astype(bf16)

    def run(chunk, g, actions):
        def body(i, carry):
            for at, action in actions.items():
                pl.when(i == at)(action)
            chunk(g, [i * UNROLL + u for u in range(UNROLL)])
            return carry

        lax.fori_loop(0, stack // LANES // UNROLL, body, 0)

    def go_on():
        hop_kv(kvb, 0, 1)
        send_kv(kvf, 1)

    def late():
        hop_sums(0)
        hop_kv(kvf, 1, 1)

    backward_actions = [
        {1: go_on},
        {1: lambda: hop_kv(kvf, 1, 0), 2: late},
    ]
    for g in range(LOCAL):
        kv_arrived(kvb, 0, g)
        kvt[...] = kvb[g].astype(f32).T.astype(bf16)
        acc[g] = jnp.zeros((total, LANES), f32)
        run(backward_chunk, g, backward_actions[g])
        send_sums(g)
    gather_heads(False)
    gq_send[...] = halves[theirs, :]
    pair_copies.append(pair_copy(3, gq_send, gq_all.at[core]))
    gq_all[core] = halves[mine, :]

    for g in range(LOCAL):
        kv_arrived(kvf, 1, g)
        kvt[...] = kvf[g].astype(f32).T.astype(bf16)
        run(forward_chunk, g, {2: lambda: hop_sums(1)} if g == 0 else {})
    gather_heads(True)
    mix_send[...] = halves[theirs, :]
    pair_copies.append(pair_copy(4, mix_send, mix_all.at[core]))
    mix_all[core] = halves[mine, :]
    pair_arrived(4, mix_all.at[other])
    made = xf[mine, :].astype(f32)
    for p in range(PAIR):
        made += mul(mix_all[p], wo[p * half : (p + 1) * half, :])
    of[...] = made.astype(bf16)

    def shift(at, src, dst, where, edge, arrive_edge):
        small = remote(
            src.at[pl.ds(0, mem)], dst.at[pl.ds(0, mem)],
            sec_send.at[at, 0], sec_recv.at[at, 0], {"section": where},
        )
        large = remote(
            src.at[pl.ds(mem, tokens)], dst.at[pl.ds(mem, tokens)],
            sec_send.at[at, 1], sec_recv.at[at, 1], {"section": where},
        )
        small.start()

        @pl.when(section != edge)
        def _():
            large.start()

        def finish():
            small.wait()

            @pl.when(section != edge)
            def _():
                large.wait_send()

            @pl.when(section != arrive_edge)
            def _():
                large.wait_recv()

        return finish

    finish_f = shift(0, of, outf_h, after, sections - 1, 0)

    for g in range(LOCAL):
        own = acc[g, pl.ds(member * rows, rows), :]
        cross = None
        for k in range(1, GROUP):
            one = source(k)

            @pl.when(is_far(one))
            def _():
                grecv[k, g] = jnp.zeros((rows, LANES), bf16)

            @pl.when(jnp.logical_not(is_far(one)))
            def _():
                place = grecv.at[k, g]
                remote(
                    place, place, gr_send.at[g, k], gr_recv.at[g, k], {"ctx": base + one}
                ).wait_recv()

            value = grecv[k, g].astype(f32)
            if k % PAIR == 0:
                own = own + value
            else:
                cross = value if cross is None else cross + value
        gsum[core * LOCAL + g] = own
        gsum[other * LOCAL + g] = cross
    pair_arrived(3, gq_all.at[other])
    columns = [gsum[h, :, :HEAD_DIM] for h in range(KV_HEADS)]
    columns += [gsum[h, :, HEAD_DIM:] for h in range(KV_HEADS)]
    grad_kv = jnp.concatenate(columns, axis=1).astype(bf16)
    grad_normed = mul(grad_kv, wkv[...], NT)
    for p in range(PAIR):
        grad_normed += mul(gq_all[p], wq[:, p * half : (p + 1) * half], NT)
    values, scale = norm(xb[mine, :])
    plain = values * scale
    pushed = gain * grad_normed
    grad_in = cot[mine, :].astype(f32) + scale * (
        pushed - plain * jnp.mean(pushed * plain, axis=-1, keepdims=True)
    )
    ob[...] = grad_in.astype(bf16)
    finish_b = shift(1, ob, outb_h, before, 0, sections - 1)

    for copy in pair_copies:
        copy.wait_send()
    finish_kv(kvb, 0)
    finish_kv(kvf, 1)
    for g in range(LOCAL):
        finish_sums(g)
    finish_f()
    finish_b()


def shards(fwd_in, bwd_saved, bwd_cot, new_tokens, loss_cot, gain, w_query, w_keyval, w_out):
    section_now = lax.axis_index("section")
    sections = lax.axis_size("section")
    rows, width = fwd_in.shape[1:]
    mem = rows - new_tokens.shape[0]
    both = PAIR * rows
    total = GROUP * rows
    stack = SHARED * both
    half = width // PAIR
    anywhere = pl.BlockSpec(memory_space=pl.ANY)
    block = jax.ShapeDtypeStruct((rows, width), bf16)
    vmem = pltpu.VMEM
    dma = pltpu.SemaphoreType.DMA
    arrived, returned = pl.pallas_call(
        functools.partial(kernel, sections, mem),
        out_shape=(block, block),
        in_specs=[anywhere] * 3 + [pl.BlockSpec(memory_space=pltpu.VMEM)] + [anywhere] * 3,
        out_specs=(anywhere, anywhere),
        scratch_shapes=[
            vmem((both, width), bf16), vmem((both, width), bf16), vmem((both, width), bf16),
            vmem(w_query.shape[1:], bf16), vmem(w_keyval.shape[1:], bf16), vmem(w_out.shape[1:], bf16),
            vmem((both, width), bf16),
            vmem((LOCAL, total, LANES), bf16), vmem((LOCAL, total, LANES), bf16),
            vmem((LANES, total), bf16),
            vmem((LOCAL, stack, LANES), bf16), vmem((LOCAL, stack, LANES), bf16),
            vmem((LOCAL, stack, LANES), bf16),
            vmem((total, LANES), jnp.int32),
            vmem((UNROLL, total, 2 * LANES), f32), vmem((UNROLL, total, LANES), f32),
            vmem((total, UNROLL * 2 * LANES), bf16),
            vmem((LOCAL, total, LANES), f32), vmem((LOCAL, total, LANES), bf16),
            vmem((GROUP, LOCAL, rows, LANES), bf16), vmem((LOCAL, both, LANES), bf16),
            vmem((KV_HEADS, rows, LANES), f32), vmem((2, KV_HEADS, rows, LANES), bf16),
            vmem((LOCAL, stack, LANES), f32), vmem((both, half), bf16),
            vmem((rows, half), bf16), vmem((PAIR, rows, half), bf16),
            vmem((rows, half), bf16), vmem((PAIR, rows, half), bf16),
            vmem((rows, width), bf16), vmem((rows, width), bf16),
            dma((6,)), dma((5,)), dma((5,)),
            dma((2, LOCAL, GROUP)), dma((2, LOCAL, GROUP)),
            dma((LOCAL, GROUP)), dma((LOCAL, GROUP)),
            dma((2, 2)), dma((2, 2)),
            dma((3, LOCAL)), dma((3, LOCAL)),
        ],
        compiler_params=pltpu.CompilerParams(
            collective_id=0, has_side_effects=True, vmem_limit_bytes=60 * 1024 * 1024
        ),
    )(fwd_in[0], bwd_saved[0], bwd_cot[0], gain, w_query[0], w_keyval[0], w_out[0])
    token_row = lax.broadcasted_iota(jnp.int32, (rows, 1), 0) >= mem
    edge = jnp.pad(new_tokens, ((mem, 0), (0, 0)))
    fwd_next = jnp.where(token_row & (section_now == 0), edge, arrived)[None]
    edge = jnp.pad(loss_cot, ((mem, 0), (0, 0)))
    cot_next = jnp.where(token_row & (section_now == sections - 1), edge, returned)[None]
    return (fwd_next, cot_next)


def solution(mesh):
    return jax.shard_map(
        shards,
        mesh=mesh,
        in_specs=(
            P("section", "ctx", None),
            P("section", "ctx", None),
            P("section", "ctx", None),
            P("ctx", None),
            P("ctx", None),
            P("section", None),
            P("section", None, None),
            P("section", None, None),
            P("section", None, None),
        ),
        out_specs=(P("section", "ctx", None), P("section", "ctx", None)),
        check_vma=False,
    )
```

```python
import functools

import jax
import jax.numpy as jnp
from jax import lax
from jax.experimental import pallas as pl
from jax.experimental.pallas import tpu as pltpu
from jax.sharding import PartitionSpec as P

HEADS = 16
KV_HEADS = 4
HEAD_DIM = 64
GROUP = 8
PAIR = 2
CHIPS = GROUP // PAIR
LOCAL = KV_HEADS // PAIR
SHARED = HEADS // KV_HEADS
LANES = 128
PIECES = 4
UNROLL = 3

epsilon = 1e-05
far = 1 << 30

bf16 = jnp.bfloat16
f32 = jnp.float32
NT = (((1,), (1,)), ((), ()))
NN = (((1,), (0,)), ((), ()))


def mul(a, b, dims=NN):
    return lax.dot_general(a, b, dims, preferred_element_type=f32)


def kernel(
    sections, mem,
    xf_h, xb_h, cot_h, gain_ref, wq_h, wkv_h, wo_h,
    outf_h, outb_h,
    xf, xb, cot, wq, wkv, wo, normed, kvf, kvb, kvt, qf, qb, gb, kpos,
    sd, ex, cat, acc, gsend, grecv, gpass, gsum, kvown, stacked, halves, gq_send, gq_all, mix_send, mix_all,
    of, ob,
    local_sem, pair_send, pair_recv, kv_send, kv_recv, gr_send, gr_recv, sec_send, sec_recv,
    hop_send, hop_recv,
):
    rows = xf_h.shape[0]
    width = xf_h.shape[1]
    both = PAIR * rows
    total = GROUP * rows
    stack = SHARED * both
    half = width // PAIR
    tokens = rows - mem

    ctx = lax.axis_index("ctx")
    section = lax.axis_index("section")
    member = lax.rem(ctx, GROUP)
    base = ctx - member
    core = lax.rem(member, PAIR)
    chip = member // PAIR
    other = 1 - core
    partner = base + chip * PAIR + other

    loads = []
    mine = pl.ds(core * rows, rows)
    for at, (src, dst) in enumerate(
        [
            (xb_h, xb.at[mine]), (wkv_h, wkv), (xf_h, xf.at[mine]),
            (wq_h, wq), (cot_h, cot.at[mine]), (wo_h, wo),
        ]
    ):
        copy = pltpu.make_async_copy(src, dst, local_sem.at[at])
        copy.start()
        loads.append(copy)
    load_xb, load_wkv, load_xf, load_wq, load_cot, load_wo = loads

    after = lax.rem(section + 1, sections)
    before = lax.rem(section + sections - 1, sections)
    barrier = pltpu.get_barrier_semaphore()
    for k in range(1, GROUP):
        pl.semaphore_signal(
            barrier, inc=1, device_id={"ctx": base + lax.rem(member + k, GROUP)},
            device_id_type=pl.DeviceIdType.MESH,
        )
    for neighbour in (after, before):
        pl.semaphore_signal(
            barrier, inc=1, device_id={"section": neighbour},
            device_id_type=pl.DeviceIdType.MESH,
        )
    pl.semaphore_wait(barrier, GROUP + 1)

    def remote(src, dst, send, recv, where):
        return pltpu.make_async_remote_copy(
            src_ref=src, dst_ref=dst, send_sem=send, recv_sem=recv,
            device_id=where, device_id_type=pl.DeviceIdType.MESH,
        )

    theirs = pl.ds(other * rows, rows)

    def pair_copy(at, src, dst):
        copy = remote(src, dst, pair_send.at[at], pair_recv.at[at], {"ctx": partner})
        copy.start()
        return copy

    pair_copies = [
        pair_copy(0, xb_h, xb.at[mine]),
        pair_copy(1, xf_h, xf.at[mine]),
        pair_copy(2, cot_h, cot.at[mine]),
    ]

    def pair_arrived(at, dst):
        remote(dst, dst, pair_send.at[at], pair_recv.at[at], {"ctx": partner}).wait_recv()

    for b in range(GROUP):
        inner = lax.broadcasted_iota(jnp.int32, (rows, LANES), 0)
        kpos[b * rows : (b + 1) * rows, :] = jnp.where(
            inner < mem, -1, b * tokens + inner - mem
        )

    gain = gain_ref[...].astype(f32)

    def norm(x):
        values = x.astype(f32)
        scale = lax.rsqrt(jnp.mean(values * values, axis=-1, keepdims=True) + epsilon)
        return values, scale

    def make_normed(x_ref, place):
        values, scale = norm(x_ref[place, :])
        normed[place, :] = (values * scale * gain).astype(bf16)

    last = CHIPS - 1
    is_end = jnp.logical_or(chip == 0, chip == last)
    is_middle = jnp.logical_not(is_end)
    opposite = last - chip
    hop_from = jnp.where(chip == 1, last, 0)
    hop_to = last - hop_from
    sum_via = jnp.where(chip == 0, 1, last - 1)
    sum_from = jnp.where(chip == 1, 0, last)

    def peer(k):
        return lax.rem(member + k, GROUP)

    def source(k):
        return lax.rem(member + GROUP - k, GROUP)

    def is_far(one):
        return jnp.logical_and(is_end, one // PAIR == opposite)

    order = sorted(range(1, GROUP), key=lambda k: abs(k - GROUP // 2))

    def project_kv(kv_ref, kind):
        keyval = mul(normed[mine, :], wkv[...])
        for h in range(KV_HEADS):
            at = h * HEAD_DIM
            after_keys = KV_HEADS * HEAD_DIM + at
            kvown[kind, h] = jnp.concatenate(
                [keyval[:, at : at + HEAD_DIM], keyval[:, after_keys : after_keys + HEAD_DIM]],
                axis=1,
            ).astype(bf16)
        for g in range(LOCAL):
            kv_ref[g, pl.ds(member * rows, rows), :] = kvown[kind, core * LOCAL + g]

    def kv_copy(kv_ref, kind, g, k):
        to = peer(k)
        return remote(
            kvown.at[kind, lax.rem(to, PAIR) * LOCAL + g],
            kv_ref.at[g, pl.ds(member * rows, rows)],
            kv_send.at[kind, g, k], kv_recv.at[kind, g, k], {"ctx": base + to},
        )

    def send_kv(kv_ref, kind):
        for g in range(LOCAL):
            for k in order:
                @pl.when(jnp.logical_not(is_far(peer(k))))
                def _():
                    kv_copy(kv_ref, kind, g, k).start()

    def finish_kv(kv_ref, kind):
        for g in range(LOCAL):
            for k in order:
                @pl.when(jnp.logical_not(is_far(peer(k))))
                def _():
                    kv_copy(kv_ref, kind, g, k).wait_send()

            @pl.when(is_middle)
            def _():
                hop_copy(kv_ref, kind, g).wait_send()

    def hop_copy(kv_ref, kind, g):
        place = kv_ref.at[g, pl.ds(hop_from * both, both)]
        return remote(
            place, place, hop_send.at[kind, g], hop_recv.at[kind, g],
            {"ctx": base + hop_to * PAIR + core},
        )

    def kv_wait(kv_ref, kind, g, one):
        k = lax.rem(member + GROUP - one, GROUP)
        place = kv_ref.at[g, pl.ds(one * rows, rows)]
        remote(
            place, place, kv_send.at[kind, g, k], kv_recv.at[kind, g, k], {"ctx": base + one}
        ).wait_recv()

    def hop_kv(kv_ref, kind, g):
        @pl.when(is_middle)
        def _():
            for c in range(PAIR):
                kv_wait(kv_ref, kind, g, hop_from * PAIR + c)
            hop_copy(kv_ref, kind, g).start()

    def kv_arrived(kv_ref, kind, g):
        for k in range(1, GROUP):
            one = source(k)
            done = jnp.logical_and(is_middle, one // PAIR == hop_from)

            @pl.when(jnp.logical_not(jnp.logical_or(is_far(one), done)))
            def _():
                kv_wait(kv_ref, kind, g, one)

        @pl.when(is_end)
        def _():
            place = kv_ref.at[g, pl.ds(opposite * both, both)]
            remote(
                place, place, hop_send.at[kind, g], hop_recv.at[kind, g],
                {"ctx": base + opposite * PAIR + core},
            ).wait_recv()

    def gr_copy(g, k):
        to = peer(k)
        return remote(
            gsend.at[g, pl.ds(to * rows, rows)], grecv.at[k, g],
            gr_send.at[g, k], gr_recv.at[g, k], {"ctx": base + to},
        )

    def is_summed(one):
        return jnp.logical_and(is_middle, one // PAIR == last - sum_from)

    def sum_copy(g, where):
        return remote(
            gsend.at[g, pl.ds(opposite * both, both)], gpass.at[g],
            hop_send.at[2, g], hop_recv.at[2, g], {"ctx": base + where * PAIR + core},
        )

    def send_sums(g):
        gsend[g] = acc[g].astype(bf16)

        @pl.when(is_end)
        def _():
            sum_copy(g, sum_via).start()

        for k in order:
            to = peer(k)

            @pl.when(jnp.logical_not(jnp.logical_or(is_far(to), is_summed(to))))
            def _():
                gr_copy(g, k).start()

    def hop_sums(g):
        @pl.when(is_middle)
        def _():
            sum_copy(g, sum_from).wait_recv()
            place = pl.ds((last - sum_from) * both, both)
            gsend[g, place, :] = (acc[g, place, :] + gpass[g].astype(f32)).astype(bf16)
            for k in order:
                @pl.when(is_summed(peer(k)))
                def _():
                    gr_copy(g, k).start()

    def finish_sums(g):
        @pl.when(is_end)
        def _():
            sum_copy(g, sum_via).wait_send()

        for k in order:
            @pl.when(jnp.logical_not(is_far(peer(k))))
            def _():
                gr_copy(g, k).wait_send()

    def spread(matrix, dst, upper, factor):
        rounded = matrix.astype(bf16).astype(f32) * factor
        zero = jnp.zeros((both, HEAD_DIM), f32)
        for g in range(LOCAL):
            for h in range(SHARED):
                at = (g * SHARED + h) * HEAD_DIM
                piece = rounded[:, at : at + HEAD_DIM]
                parts = [zero, piece] if upper else [piece, zero]
                dst[g, h * both : (h + 1) * both, :] = jnp.concatenate(parts, axis=1).astype(bf16)

    scale_by = HEAD_DIM ** (-0.5)
    my_cols = pl.ds(pl.multiple_of(core * half, half), half)

    load_xb.wait()
    make_normed(xb, mine)
    load_wkv.wait()
    project_kv(kvb, 0)
    send_kv(kvb, 0)
    pair_arrived(0, xb.at[theirs])
    make_normed(xb, theirs)
    load_wq.wait()
    spread(mul(normed[...], wq[:, my_cols]), qb, False, scale_by)
    load_cot.wait()
    pair_arrived(2, cot.at[theirs])
    load_wo.wait()
    spread(mul(cot[...], wo[my_cols, :], NT), gb, True, 1.0)
    load_xf.wait()
    make_normed(xf, mine)
    project_kv(kvf, 1)
    hop_kv(kvb, 0, 0)
    pair_arrived(1, xf.at[theirs])
    make_normed(xf, theirs)
    spread(mul(normed[...], wq[:, my_cols]), qf, False, scale_by)

    step = total // PIECES

    def query_positions(start):
        row = start + lax.broadcasted_iota(jnp.int32, (1, LANES), 1)
        for h in range(1, SHARED):
            row = jnp.where(row >= both, row - both, row)
        block = jnp.where(row >= rows, 1, 0)
        inner = row - block * rows
        return jnp.where(inner < mem, far, (chip * PAIR + block) * tokens + inner - mem)

    parts = [slice(p * step, (p + 1) * step) for p in range(PIECES)]

    def backward_chunk(g, chunks):
        starts = [pl.multiple_of(i * LANES, LANES) for i in chunks]
        pairs = [
            jnp.concatenate([qb[g, pl.ds(at, LANES), :], gb[g, pl.ds(at, LANES), :]], axis=0)
            for at in starts
        ]
        for u, start in enumerate(starts):
            position = query_positions(start)
            top = None
            for part in parts:
                product = mul(kvb[g, part, :], pairs[u], NT)
                scores = jnp.where(kpos[part, :] <= position, product[:, :LANES], -1e30)
                sd[u, part, :LANES] = scores
                sd[u, part, LANES:] = product[:, LANES:]
                peak = jnp.max(scores, axis=0, keepdims=True)
                top = peak if top is None else jnp.maximum(top, peak)
            norm_sum = jnp.zeros((1, LANES), f32)
            delta = jnp.zeros((1, LANES), f32)
            for part in parts:
                expd = jnp.exp(sd[u, part, :LANES] - top)
                ex[u, part, :] = expd
                norm_sum += jnp.sum(expd, axis=0, keepdims=True)
                delta += jnp.sum(expd * sd[u, part, LANES:], axis=0, keepdims=True)
            inverse = 1.0 / norm_sum
            delta = delta * inverse
            at = u * 2 * LANES
            for part in parts:
                probs = ex[u, part, :] * inverse
                cat[part, at + LANES : at + 2 * LANES] = probs.astype(bf16)
                cat[part, at : at + LANES] = (probs * (sd[u, part, LANES:] - delta)).astype(bf16)
        everything = jnp.concatenate(pairs, axis=0)
        for part in parts:
            acc[g, part, :] += mul(cat[part, :], everything)
        for u, start in enumerate(starts):
            at = u * 2 * LANES
            turned = mul(kvt[...], cat[:, at : at + LANES])
            stacked[g, pl.ds(start, LANES), :] = turned.T * scale_by

    def forward_chunk(g, chunks):
        for u, i in enumerate(chunks):
            start = pl.multiple_of(i * LANES, LANES)
            queries = qf[g, pl.ds(start, LANES), :]
            position = query_positions(start)
            top = None
            for part in parts:
                product = mul(kvf[g, part, :], queries, NT)
                scores = jnp.where(kpos[part, :] <= position, product, -1e30)
                sd[u, part, :LANES] = scores
                peak = jnp.max(scores, axis=0, keepdims=True)
                top = peak if top is None else jnp.maximum(top, peak)
            norm_sum = jnp.zeros((1, LANES), f32)
            for part in parts:
                expd = jnp.exp(sd[u, part, :LANES] - top)
                ex[u, part, :] = expd
                norm_sum += jnp.sum(expd, axis=0, keepdims=True)
            inverse = 1.0 / norm_sum
            for part in parts:
                cat[part, u * LANES : (u + 1) * LANES] = (ex[u, part, :] * inverse).astype(bf16)
        turned = mul(kvt[...], cat[:, : len(chunks) * LANES])
        for u, i in enumerate(chunks):
            start = pl.multiple_of(i * LANES, LANES)
            stacked[g, pl.ds(start, LANES), :] = turned[:, u * LANES : (u + 1) * LANES].T

    def gather_heads(upper):
        first = HEAD_DIM if upper else 0
        lanes = slice(first, first + HEAD_DIM)
        for g in range(LOCAL):
            for h in range(0, SHARED, 2):
                left = stacked[g, h * both : (h + 1) * both, lanes]
                right = stacked[g, (h + 1) * both : (h + 2) * both, lanes]
                at = (g * SHARED + h) * HEAD_DIM
                halves[:, at : at + LANES] = jnp.concatenate([left, right], axis=1).astype(bf16)

    def run(chunk, g, actions):
        def body(i, carry):
            for at, action in actions.items():
                pl.when(i == at)(action)
            chunk(g, [i * UNROLL + u for u in range(UNROLL)])
            return carry

        lax.fori_loop(0, stack // LANES // UNROLL, body, 0)

    def go_on():
        hop_kv(kvb, 0, 1)
        send_kv(kvf, 1)

    def late():
        hop_sums(0)
        hop_kv(kvf, 1, 1)

    backward_actions = [
        {1: go_on},
        {1: lambda: hop_kv(kvf, 1, 0), 2: late},
    ]
    for g in range(LOCAL):
        kv_arrived(kvb, 0, g)
        kvt[...] = kvb[g].astype(f32).T.astype(bf16)
        acc[g] = jnp.zeros((total, LANES), f32)
        run(backward_chunk, g, backward_actions[g])
        send_sums(g)
    gather_heads(False)
    gq_send[...] = halves[theirs, :]
    pair_copies.append(pair_copy(3, gq_send, gq_all.at[core]))
    gq_all[core] = halves[mine, :]

    for g in range(LOCAL):
        kv_arrived(kvf, 1, g)
        kvt[...] = kvf[g].astype(f32).T.astype(bf16)
        run(forward_chunk, g, {2: lambda: hop_sums(1)} if g == 0 else {})
    gather_heads(True)
    mix_send[...] = halves[theirs, :]
    pair_copies.append(pair_copy(4, mix_send, mix_all.at[core]))
    mix_all[core] = halves[mine, :]
    pair_arrived(4, mix_all.at[other])
    made = xf[mine, :].astype(f32)
    for p in range(PAIR):
        made += mul(mix_all[p], wo[p * half : (p + 1) * half, :])
    of[...] = made.astype(bf16)

    def shift(at, src, dst, where, edge, arrive_edge):
        small = remote(
            src.at[pl.ds(0, mem)], dst.at[pl.ds(0, mem)],
            sec_send.at[at, 0], sec_recv.at[at, 0], {"section": where},
        )
        large = remote(
            src.at[pl.ds(mem, tokens)], dst.at[pl.ds(mem, tokens)],
            sec_send.at[at, 1], sec_recv.at[at, 1], {"section": where},
        )
        small.start()

        @pl.when(section != edge)
        def _():
            large.start()

        def finish():
            small.wait()

            @pl.when(section != edge)
            def _():
                large.wait_send()

            @pl.when(section != arrive_edge)
            def _():
                large.wait_recv()

        return finish

    finish_f = shift(0, of, outf_h, after, sections - 1, 0)
    pair_arrived(3, gq_all.at[other])
    from_queries = mul(gq_all[0], wq[:, :half], NT)
    for p in range(1, PAIR):
        from_queries += mul(gq_all[p], wq[:, p * half : (p + 1) * half], NT)
    values, scale = norm(xb[mine, :])
    plain = values * scale

    for g in range(LOCAL):
        own = acc[g, pl.ds(member * rows, rows), :]
        cross = None
        for k in range(1, GROUP):
            one = source(k)

            @pl.when(is_far(one))
            def _():
                grecv[k, g] = jnp.zeros((rows, LANES), bf16)

            @pl.when(jnp.logical_not(is_far(one)))
            def _():
                place = grecv.at[k, g]
                remote(
                    place, place, gr_send.at[g, k], gr_recv.at[g, k], {"ctx": base + one}
                ).wait_recv()

            value = grecv[k, g].astype(f32)
            if k % PAIR == 0:
                own = own + value
            else:
                cross = value if cross is None else cross + value
        gsum[core * LOCAL + g] = own
        gsum[other * LOCAL + g] = cross
    columns = [gsum[h, :, :HEAD_DIM] for h in range(KV_HEADS)]
    columns += [gsum[h, :, HEAD_DIM:] for h in range(KV_HEADS)]
    grad_kv = jnp.concatenate(columns, axis=1).astype(bf16)
    grad_normed = from_queries + mul(grad_kv, wkv[...], NT)
    pushed = gain * grad_normed
    grad_in = cot[mine, :].astype(f32) + scale * (
        pushed - plain * jnp.mean(pushed * plain, axis=-1, keepdims=True)
    )
    ob[...] = grad_in.astype(bf16)
    finish_b = shift(1, ob, outb_h, before, 0, sections - 1)

    for copy in pair_copies:
        copy.wait_send()
    finish_kv(kvb, 0)
    finish_kv(kvf, 1)
    for g in range(LOCAL):
        finish_sums(g)
    finish_f()
    finish_b()


def shards(fwd_in, bwd_saved, bwd_cot, new_tokens, loss_cot, gain, w_query, w_keyval, w_out):
    section_now = lax.axis_index("section")
    sections = lax.axis_size("section")
    rows, width = fwd_in.shape[1:]
    mem = rows - new_tokens.shape[0]
    both = PAIR * rows
    total = GROUP * rows
    stack = SHARED * both
    half = width // PAIR
    anywhere = pl.BlockSpec(memory_space=pl.ANY)
    block = jax.ShapeDtypeStruct((rows, width), bf16)
    vmem = pltpu.VMEM
    dma = pltpu.SemaphoreType.DMA
    arrived, returned = pl.pallas_call(
        functools.partial(kernel, sections, mem),
        out_shape=(block, block),
        in_specs=[anywhere] * 3 + [pl.BlockSpec(memory_space=pltpu.VMEM)] + [anywhere] * 3,
        out_specs=(anywhere, anywhere),
        scratch_shapes=[
            vmem((both, width), bf16), vmem((both, width), bf16), vmem((both, width), bf16),
            vmem(w_query.shape[1:], bf16), vmem(w_keyval.shape[1:], bf16), vmem(w_out.shape[1:], bf16),
            vmem((both, width), bf16),
            vmem((LOCAL, total, LANES), bf16), vmem((LOCAL, total, LANES), bf16),
            vmem((LANES, total), bf16),
            vmem((LOCAL, stack, LANES), bf16), vmem((LOCAL, stack, LANES), bf16),
            vmem((LOCAL, stack, LANES), bf16),
            vmem((total, LANES), jnp.int32),
            vmem((UNROLL, total, 2 * LANES), f32), vmem((UNROLL, total, LANES), f32),
            vmem((total, UNROLL * 2 * LANES), bf16),
            vmem((LOCAL, total, LANES), f32), vmem((LOCAL, total, LANES), bf16),
            vmem((GROUP, LOCAL, rows, LANES), bf16), vmem((LOCAL, both, LANES), bf16),
            vmem((KV_HEADS, rows, LANES), f32), vmem((2, KV_HEADS, rows, LANES), bf16),
            vmem((LOCAL, stack, LANES), f32), vmem((both, half), bf16),
            vmem((rows, half), bf16), vmem((PAIR, rows, half), bf16),
            vmem((rows, half), bf16), vmem((PAIR, rows, half), bf16),
            vmem((rows, width), bf16), vmem((rows, width), bf16),
            dma((6,)), dma((5,)), dma((5,)),
            dma((2, LOCAL, GROUP)), dma((2, LOCAL, GROUP)),
            dma((LOCAL, GROUP)), dma((LOCAL, GROUP)),
            dma((2, 2)), dma((2, 2)),
            dma((3, LOCAL)), dma((3, LOCAL)),
        ],
        compiler_params=pltpu.CompilerParams(
            collective_id=0, has_side_effects=True, vmem_limit_bytes=60 * 1024 * 1024
        ),
    )(fwd_in[0], bwd_saved[0], bwd_cot[0], gain, w_query[0], w_keyval[0], w_out[0])
    token_row = lax.broadcasted_iota(jnp.int32, (rows, 1), 0) >= mem
    edge = jnp.pad(new_tokens, ((mem, 0), (0, 0)))
    fwd_next = jnp.where(token_row & (section_now == 0), edge, arrived)[None]
    edge = jnp.pad(loss_cot, ((mem, 0), (0, 0)))
    cot_next = jnp.where(token_row & (section_now == sections - 1), edge, returned)[None]
    return (fwd_next, cot_next)


def solution(mesh):
    return jax.shard_map(
        shards,
        mesh=mesh,
        in_specs=(
            P("section", "ctx", None),
            P("section", "ctx", None),
            P("section", "ctx", None),
            P("ctx", None),
            P("ctx", None),
            P("section", None),
            P("section", None, None),
            P("section", None, None),
            P("section", None, None),
        ),
        out_specs=(P("section", "ctx", None), P("section", "ctx", None)),
        check_vma=False,
    )
```
